32 devices in a mesh: frm: 4 (over z), vox: 8 (over y, x, core).
Axes of the slice: x: 2, y: 2, z: 4, core: 2. Of those that a mesh axis runs over, the one named last changes fastest.
Arguments:
- movie_matrix: bfloat16 [8192, 16384], P('frm', 'vox'), may hold values from -8 to 8
- voxel_probe: bfloat16 [16384, 64], P('vox'), may hold values from -0.046875 to 0.046875
- frame_probe: bfloat16 [8192, 64], P('frm'), may hold values from -0.0625 to 0.0625
Outputs:
- lowrank: bfloat16 [8192, 16384], P('frm', 'vox')
- sparse: bfloat16 [8192, 16384], P('frm', 'vox')
The draws below stay inside these ranges and needn't reach their ends.
All inputs are finite; a program needn't handle non-finite values.
Results may differ from the reference program's by a relative error of at most 0.04.
Values may be sent and summed in bfloat16 or wider, within the bound.
No kernel may reach another device: no remote copies, remote signals or barrier semaphores. Data moves between devices by JAX's collectives and lax.ppermute only.
A program may use at most 128 MiB of HBM per device.

```python
import jax
import jax.numpy as jnp
from jax import lax

RANK = 64
ITERS = 2
FRAMES = 8192
VOXELS = 16384


signal_rank = 96


def draw_movie_matrix(key, part):
    keys = jax.random.split(jax.random.fold_in(key, 17), 6)
    basis_left = jax.random.normal(keys[0], (FRAMES, signal_rank), jnp.float32)
    basis_right = jax.random.normal(keys[1], (VOXELS, signal_rank), jnp.float32)
    signal = jnp.dot(basis_left, basis_right.T, precision=lax.Precision.HIGHEST) / jnp.sqrt(float(signal_rank))
    spike_mask = jax.random.bernoulli(keys[2], 0.05, (FRAMES, VOXELS)).astype(jnp.float32)
    spike_sign = 2.0 * jax.random.bernoulli(keys[3], 0.5, (FRAMES, VOXELS)).astype(jnp.float32) - 1.0
    spike_size = jax.random.uniform(keys[4], (FRAMES, VOXELS), jnp.float32, 2.0, 4.0)
    noise = 0.3 * jax.random.normal(keys[5], (FRAMES, VOXELS), jnp.float32)
    movie = signal + noise + spike_mask * spike_sign * spike_size
    return jnp.clip(movie, -8.0, 8.0).astype(jnp.bfloat16)


def level_of(own_key, extent, cuts, low, top_value):
    gain, own = 1.0, jax.random.fold_in(own_key, 6)
    for dim, shards_of in cuts:
        heights = jnp.exp(jax.random.uniform(jax.random.fold_in(own, dim), (shards_of,), jnp.float32, low / len(cuts), top_value / len(cuts)))
        gain = gain * jnp.repeat(heights, extent[dim] // shards_of).reshape([-1 if axis == dim else 1 for axis in range(len(extent))])
    return gain


def normal_values(own_key, extent, scale, limit, cuts=(), kind=jnp.bfloat16):
    drawn = scale * jax.random.normal(own_key, extent, jnp.float32)
    if cuts:
        drawn = drawn * level_of(own_key, extent, cuts, -0.22, 0.18)
    return jnp.clip(drawn, -limit, limit).astype(kind)


def setup_inputs(seed: int = 0) -> dict:
    seeds = jax.random.split(jax.random.key(seed), 4)
    return {
        "movie_matrix": draw_movie_matrix(jax.random.fold_in(seeds[3], 71), 0),
        "voxel_probe": normal_values(seeds[1], (VOXELS, RANK), VOXELS ** -0.5, 0.046875, ((0, 8),)),
        "frame_probe": normal_values(seeds[2], (FRAMES, RANK), FRAMES ** -0.5, 0.0625, ((0, 4),)),
    }


cutoff = 1.0
ridge_scale = 0.1

def core_map(core_matrix):
    gram_matrix = jnp.dot(core_matrix.T.astype(jnp.float32), core_matrix.astype(jnp.float32), precision=lax.Precision.HIGHEST, preferred_element_type=jnp.float32)
    core_order = core_matrix.shape[0]
    ridge_shift = ridge_scale * (jnp.trace(gram_matrix) / core_order + 1e-06)
    factor = jnp.linalg.cholesky(gram_matrix + ridge_shift * jnp.eye(core_order, dtype=jnp.float32))
    return jax.scipy.linalg.cho_solve((factor, True), core_matrix.T)

def shrink(values):
    return jnp.sign(values) * jnp.maximum(jnp.abs(values) - cutoff, 0.0)

def reference(movie_matrix, voxel_probe, frame_probe):
    sparse = jnp.zeros_like(movie_matrix)
    probe_wide = frame_probe.astype(jnp.float32)
    lowrank = jnp.zeros(movie_matrix.shape, jnp.float32)
    for iteration in range(ITERS):
        current = (movie_matrix.astype(jnp.float32) - sparse.astype(jnp.float32)).astype(jnp.bfloat16)
        frame_sketch = jnp.dot(current.astype(jnp.float32), voxel_probe.astype(jnp.float32), preferred_element_type=jnp.float32)
        voxel_sketch = lax.dot_general(current.astype(jnp.float32), frame_probe.astype(jnp.float32), (((0,), (0,)), ((), ())), preferred_element_type=jnp.float32)
        core_matrix = lax.dot_general(probe_wide.astype(jnp.float32), frame_sketch.astype(jnp.float32), (((0,), (0,)), ((), ())), precision=lax.Precision.HIGHEST, preferred_element_type=jnp.float32)
        core_mixer = core_map(core_matrix)
        left_factor = jnp.dot(frame_sketch.astype(jnp.float32), core_mixer.astype(jnp.float32), precision=lax.Precision.HIGHEST, preferred_element_type=jnp.float32).astype(jnp.bfloat16)
        right_factor = voxel_sketch.astype(jnp.bfloat16)
        lowrank = lax.dot_general(left_factor.astype(jnp.float32), right_factor.astype(jnp.float32), (((1,), (1,)), ((), ())), preferred_element_type=jnp.float32)
        sparse = shrink(movie_matrix.astype(jnp.float32) - lowrank).astype(jnp.bfloat16)
    return (lowrank.astype(jnp.bfloat16), sparse)
```

```python
import functools

import jax
import jax.numpy as jnp
from jax import lax
from jax.experimental import pallas as pl
from jax.experimental.pallas import tpu as pltpu
from jax.sharding import PartitionSpec as P

ITERS = 2
cutoff = 1.0
ridge_scale = 0.1


F32 = jnp.float32
BF16 = jnp.bfloat16
LANES = 128


def dot(a, b, contract=((1,), (0,))):
    return lax.dot_general(a, b, (contract, ((), ())), preferred_element_type=F32)


def split2(x):
    high = x.astype(BF16)
    return high, (x - high.astype(F32)).astype(BF16)


def pack_core(core):
    high, low = split2(core)
    return jnp.concatenate([high, low], axis=1)


def unpack_core(packed):
    rank = packed.shape[0]
    wide = packed.astype(F32)
    return wide[:, :rank] + wide[:, rank:]


def finish_sketch(where_ref, y1_scr, y2_scr, vp_ref, own_ref, send_ref, y2_refs):
    rank, frames = y1_scr.shape
    half = frames // 2
    peers = len(y2_refs)
    share = y2_scr.shape[1] // peers
    y2 = y2_scr[...]
    high, rest = split2(y2)
    low = (y2 - high.astype(F32) - rest.astype(F32)).astype(BF16)
    vp = vp_ref[...]
    core = dot(high, vp) + dot(rest, vp) + dot(low, vp)
    side = where_ref[0]
    row = where_ref[1]
    own_ref[:, :half] = y1_scr[:, pl.ds(pl.multiple_of(side * half, LANES), half)]
    own_ref[:, half : half + 2 * rank] = jnp.concatenate([core, jnp.zeros_like(core)], axis=1)
    other = y1_scr[:, pl.ds(pl.multiple_of((1 - side) * half, LANES), half)]
    send_ref[:, :half] = other.astype(BF16)
    send_ref[:, half : half + 2 * rank] = pack_core(core)
    for k in range(peers):
        slot = jnp.bitwise_xor(row, k)
        part = y2_scr[:, pl.ds(pl.multiple_of(slot * share, LANES), share)]
        y2_refs[k][...] = part.astype(y2_refs[k].dtype)


def add_block(cur, step, rows, cols, fp, vp_ref, y1, y2_scr):
    y2_scr[:, cols] += dot(fp, cur, ((0,), (0,)))
    part = dot(cur, vp_ref[cols, :])
    return part if y1 is None else y1 + part


def first_kernel(where_ref, movie_ref, vp_ref, fp_ref, own_ref, send_ref, *rest):
    *y2_refs, y1_scr, y2_scr = rest
    step = pl.program_id(0)
    rows = movie_ref.shape[0]

    @pl.when(step == 0)
    def _():
        y2_scr[...] = jnp.zeros_like(y2_scr)

    cur = movie_ref[...]
    y2_scr[...] += dot(fp_ref[...], cur, ((0,), (0,)))
    y1 = dot(cur, vp_ref[...])
    y1_scr[:, pl.ds(pl.multiple_of(step * rows, LANES), rows)] = y1.T

    @pl.when(step == pl.num_programs(0) - 1)
    def _():
        finish_sketch(where_ref, y1_scr, y2_scr, vp_ref, own_ref, send_ref, y2_refs)


def pair_kernel(own_ref, got_ref, msg_ref):
    rank, width = own_ref.shape
    half = width - 2 * rank
    msg_ref[:, :half] = (own_ref[:, :half] + got_ref[:, :half].astype(F32)).astype(BF16)
    core = own_ref[:, half:][:, :rank] + unpack_core(got_ref[:, half:])
    msg_ref[:, half:] = pack_core(core)


def plane_kernel(n_plane, *refs):
    plane_refs = refs[:n_plane]
    *y2_refs, half_ref, zmsg_ref = refs[n_plane:]
    rank, width = plane_refs[0].shape
    half = width - 2 * rank
    share = y2_refs[0].shape[1]
    total = plane_refs[0][:, :half].astype(F32)
    core = unpack_core(plane_refs[0][:, half:])
    for ref in plane_refs[1:]:
        total += ref[:, :half].astype(F32)
        core += unpack_core(ref[:, half:])
    half_ref[...] = total.astype(BF16)
    y2 = y2_refs[0][...]
    for ref in y2_refs[1:]:
        y2 += ref[...].astype(F32)
    zmsg_ref[:, :share] = y2.astype(BF16)
    zmsg_ref[:, share:] = pack_core(core)


def solve_mixer(core):
    rank = core.shape[0]
    gram = lax.dot_general(
        core, core, (((0,), (0,)), ((), ())), precision=lax.Precision.HIGHEST, preferred_element_type=F32
    )
    r = lax.broadcasted_iota(jnp.int32, (rank, rank), 0)
    c = lax.broadcasted_iota(jnp.int32, (rank, rank), 1)
    eye = (r == c).astype(F32)
    shift = ridge_scale * (jnp.sum(gram * eye) / rank + 1e-06)
    table = jnp.concatenate([gram + shift * eye, core.T], axis=1)
    line = lax.broadcasted_iota(jnp.int32, (rank, 1), 0)
    for k in range(0, rank, 2):
        row0 = table[k : k + 1, :]
        row1 = table[k + 1 : k + 2, :]
        a, b, d = row0[:, k : k + 1], row0[:, k + 1 : k + 2], row1[:, k + 1 : k + 2]
        inv = 1.0 / (a * d - b * b)
        new0 = (row0 * d - row1 * b) * inv
        new1 = (row1 * a - row0 * b) * inv
        col0 = table[:, k : k + 1] - (line == k).astype(F32)
        col1 = table[:, k + 1 : k + 2] - (line == k + 1).astype(F32)
        table = table - col0 * new0 - col1 * new1
    return table[:, rank:]


def prologue(where_ref, half_refs, zmsg_refs, left_scr, right_scr):
    rank, share = zmsg_refs[0].shape
    share -= 2 * rank
    half = half_refs[0].shape[1]
    core = unpack_core(zmsg_refs[0][:, share:])
    for ref in zmsg_refs[1:]:
        core += unpack_core(ref[:, share:])
    mixer = solve_mixer(core)
    high, low = split2(mixer)
    side = where_ref[0]
    row = where_ref[1]
    for k in range(2):
        y1 = half_refs[k][...]
        left = dot(y1, high, ((0,), (0,))) + dot(y1, low, ((0,), (0,)))
        slot = jnp.bitwise_xor(side, k)
        left_scr[pl.ds(pl.multiple_of(slot * half, 16), half), :] = left.astype(BF16)
    for k in range(len(zmsg_refs)):
        slot = jnp.bitwise_xor(row, k)
        right_scr[:, pl.ds(pl.multiple_of(slot * share, LANES), share)] = zmsg_refs[k][:, :share]


def middle_kernel(n_row, chunk, where_ref, movie_ref, vp_ref, fp_ref, *rest):
    half_refs = rest[:2]
    zmsg_refs = rest[2 : 2 + n_row]
    own_ref, send_ref = rest[2 + n_row : 4 + n_row]
    *y2_refs, left_scr, right_scr, y1_scr, y2_scr = rest[4 + n_row :]
    step = pl.program_id(0)
    rows, voxels = movie_ref.shape

    @pl.when(step == 0)
    def _():
        prologue(where_ref, half_refs, zmsg_refs, left_scr, right_scr)
        y2_scr[...] = jnp.zeros_like(y2_scr)

    left = left_scr[pl.ds(pl.multiple_of(step * rows, 16), rows), :]
    fp = fp_ref[...]
    y1 = None
    for j in range(0, voxels, chunk):
        cols = slice(j, j + chunk)
        low = dot(left, right_scr[:, cols])
        gap = movie_ref[:, cols].astype(F32) - low
        cur = (low + jnp.clip(gap, -cutoff, cutoff)).astype(BF16)
        y2_scr[:, cols] += dot(fp, cur, ((0,), (0,)))
        part = dot(cur, vp_ref[cols, :])
        y1 = part if y1 is None else y1 + part
    y1_scr[:, pl.ds(pl.multiple_of(step * rows, LANES), rows)] = y1.T

    @pl.when(step == pl.num_programs(0) - 1)
    def _():
        finish_sketch(where_ref, y1_scr, y2_scr, vp_ref, own_ref, send_ref, y2_refs)


def last_kernel(n_row, chunk, where_ref, movie_ref, *rest):
    half_refs = rest[:2]
    zmsg_refs = rest[2 : 2 + n_row]
    low_ref, sparse_ref, left_scr, right_scr = rest[2 + n_row :]
    step = pl.program_id(0)
    rows, voxels = movie_ref.shape

    @pl.when(step == 0)
    def _():
        prologue(where_ref, half_refs, zmsg_refs, left_scr, right_scr)

    left = left_scr[pl.ds(pl.multiple_of(step * rows, 16), rows), :]
    for j in range(0, voxels, chunk):
        cols = slice(j, j + chunk)
        low = dot(left, right_scr[:, cols])
        low_ref[:, cols] = low.astype(BF16)
        gap = movie_ref[:, cols].astype(F32) - low
        sparse_ref[:, cols] = (gap - jnp.clip(gap, -cutoff, cutoff)).astype(BF16)


def whole(shape):
    return pl.BlockSpec(shape, lambda i, *_: (0,) * len(shape))


def block_rows(rows, width):
    return pl.BlockSpec((rows, width), lambda i, *_: (i, 0))


def vmem_call(kernel, outs, args, flops=1e6):
    spec = pl.BlockSpec(memory_space=pltpu.VMEM)
    moved = sum(a.size * a.dtype.itemsize for a in args) + sum(o.size * o.dtype.itemsize for o in outs)
    return pl.pallas_call(
        kernel,
        out_shape=outs,
        in_specs=[spec] * len(args),
        out_specs=[spec] * len(outs),
        compiler_params=pltpu.CompilerParams(vmem_limit_bytes=8 * 1024 * 1024),
        cost_estimate=pl.CostEstimate(flops=int(flops), bytes_accessed=int(moved), transcendentals=0),
    )(*args)


def exchange(x, axis, k):
    size = lax.axis_size(axis)
    return lax.ppermute(x, axis, [(i, i ^ k) for i in range(size)])


def on_device(movie, voxel_probe, frame_probe):
    frames, voxels = movie.shape
    rank = voxel_probe.shape[1]
    n_vox, n_row = lax.axis_size("vox"), lax.axis_size("frm")
    n_plane = n_vox // 2
    half, share = frames // 2, voxels // n_row
    width = half + 2 * rank
    rows = min(256, frames)
    chunk = min(512, voxels)
    steps = frames // rows
    where = jnp.stack([lax.axis_index("vox") % 2, lax.axis_index("frm")]).astype(jnp.int32)

    sketch_shapes = [
        jax.ShapeDtypeStruct((rank, width), F32),
        jax.ShapeDtypeStruct((rank, width), BF16),
        jax.ShapeDtypeStruct((rank, share), F32),
    ] + [jax.ShapeDtypeStruct((rank, share), BF16)] * (n_row - 1)
    sketch_specs = [whole(s.shape) for s in sketch_shapes]
    sums = [pltpu.VMEM((rank, frames), F32), pltpu.VMEM((rank, voxels), F32)]
    factors = [pltpu.VMEM((frames, rank), BF16), pltpu.VMEM((rank, voxels), BF16)]
    base_specs = [block_rows(rows, voxels)]
    probe_specs = [whole((voxels, rank)), block_rows(rows, rank)]
    side_specs = [whole((rank, half))] * 2 + [whole((rank, share + 2 * rank))] * n_row

    def run(kernel, in_specs, out_specs, out_shape, scratch, passes, args):
        return pl.pallas_call(
            kernel,
            grid_spec=pltpu.PrefetchScalarGridSpec(
                num_scalar_prefetch=1, grid=(steps,), in_specs=in_specs, out_specs=out_specs, scratch_shapes=scratch
            ),
            out_shape=out_shape,
            compiler_params=pltpu.CompilerParams(
                dimension_semantics=("arbitrary",), vmem_limit_bytes=48 * 1024 * 1024
            ),
            cost_estimate=pl.CostEstimate(
                flops=2 * passes * frames * voxels * rank, bytes_accessed=2 * frames * voxels, transcendentals=0
            ),
        )(where, *args)

    def share_sketch(own, send, y2_parts):
        got = exchange(send, "vox", 1)
        y2 = [y2_parts[0]] + [exchange(y2_parts[k], "frm", k) for k in range(1, n_row)]
        (msg,) = vmem_call(pair_kernel, [jax.ShapeDtypeStruct((rank, width), BF16)], [own, got])
        plane = [msg] + [exchange(msg, "vox", 2 * k) for k in range(1, n_plane)]
        own_half, zmsg = vmem_call(
            functools.partial(plane_kernel, n_plane),
            [
                jax.ShapeDtypeStruct((rank, half), BF16),
                jax.ShapeDtypeStruct((rank, share + 2 * rank), BF16),
            ],
            plane + y2,
        )
        zmsgs = [zmsg] + [exchange(zmsg, "frm", k) for k in range(1, n_row)]
        return [own_half, exchange(own_half, "vox", 1)] + zmsgs

    own, send, *y2_parts = run(
        first_kernel, base_specs + probe_specs, sketch_specs, sketch_shapes, sums, 2, (movie, voxel_probe, frame_probe)
    )
    sides = share_sketch(own, send, y2_parts)
    for _ in range(ITERS - 1):
        own, send, *y2_parts = run(
            functools.partial(middle_kernel, n_row, chunk),
            base_specs + probe_specs + side_specs,
            sketch_specs,
            sketch_shapes,
            factors + sums,
            3,
            (movie, voxel_probe, frame_probe, *sides),
        )
        sides = share_sketch(own, send, y2_parts)
    out = jax.ShapeDtypeStruct((frames, voxels), BF16)
    return tuple(
        run(
            functools.partial(last_kernel, n_row, chunk),
            base_specs + side_specs,
            [block_rows(rows, voxels)] * 2,
            [out, out],
            factors,
            1,
            (movie, *sides),
        )
    )


def solution(mesh):
    return jax.shard_map(
        on_device,
        mesh=mesh,
        in_specs=(P("frm", "vox"), P("vox", None), P("frm", None)),
        out_specs=(P("frm", "vox"), P("frm", "vox")),
        check_vma=False,
    )
```

```python
import functools

import jax
import jax.numpy as jnp
from jax import lax
from jax.experimental import pallas as pl
from jax.experimental.pallas import tpu as pltpu
from jax.sharding import PartitionSpec as P

ITERS = 2
cutoff = 1.0
ridge_scale = 0.1


F32 = jnp.float32
BF16 = jnp.bfloat16
LANES = 128


def dot(a, b, contract=((1,), (0,))):
    return lax.dot_general(a, b, (contract, ((), ())), preferred_element_type=F32)


def split2(x):
    high = x.astype(BF16)
    return high, (x - high.astype(F32)).astype(BF16)


def pack_core(core):
    high, low = split2(core)
    return jnp.concatenate([high, low], axis=1)


def unpack_core(packed):
    rank = packed.shape[0]
    wide = packed.astype(F32)
    return wide[:, :rank] + wide[:, rank:]


def finish_sketch(where_ref, y1_scr, y2_scr, vpt_ref, own_ref, send_ref, y2_refs):
    rank, frames = y1_scr.shape
    half = frames // 2
    peers = len(y2_refs)
    share = y2_scr.shape[1] // peers
    y2 = y2_scr[...]
    high, rest = split2(y2)
    low = (y2 - high.astype(F32) - rest.astype(F32)).astype(BF16)
    vp = vpt_ref[...]
    core = sum(dot(part, vp, ((1,), (1,))) for part in (high, rest, low))
    side = where_ref[0]
    row = where_ref[1]
    own_ref[:, :half] = y1_scr[:, pl.ds(pl.multiple_of(side * half, LANES), half)]
    own_ref[:, half : half + 2 * rank] = jnp.concatenate([core, jnp.zeros_like(core)], axis=1)
    other = y1_scr[:, pl.ds(pl.multiple_of((1 - side) * half, LANES), half)]
    send_ref[:, :half] = other.astype(BF16)
    send_ref[:, half : half + 2 * rank] = pack_core(core)
    for k in range(peers):
        slot = jnp.bitwise_xor(row, k)
        part = y2_scr[:, pl.ds(pl.multiple_of(slot * share, LANES), share)]
        y2_refs[k][...] = part.astype(y2_refs[k].dtype)


def first_kernel(where_ref, movie_ref, vpt_ref, fpt_ref, own_ref, send_ref, *rest):
    *y2_refs, y1_scr, y2_scr = rest
    step = pl.program_id(0)
    rows = movie_ref.shape[0]

    @pl.when(step == 0)
    def _():
        y2_scr[...] = jnp.zeros_like(y2_scr)

    cur = movie_ref[...]
    y2_scr[...] += dot(fpt_ref[...], cur)
    y1_scr[:, pl.ds(pl.multiple_of(step * rows, rows), rows)] = dot(vpt_ref[...], cur, ((1,), (1,)))

    @pl.when(step == pl.num_programs(0) - 1)
    def _():
        finish_sketch(where_ref, y1_scr, y2_scr, vpt_ref, own_ref, send_ref, y2_refs)


def pair_kernel(own_ref, got_ref, msg_ref):
    rank, width = own_ref.shape
    half = width - 2 * rank
    msg_ref[:, :half] = (own_ref[:, :half] + got_ref[:, :half].astype(F32)).astype(BF16)
    core = own_ref[:, half:][:, :rank] + unpack_core(got_ref[:, half:])
    msg_ref[:, half:] = pack_core(core)


def plane_kernel(*refs):
    *plane_refs, half_ref, core_ref = refs
    half = half_ref.shape[1]
    total = plane_refs[0][:, :half].astype(F32)
    core = unpack_core(plane_refs[0][:, half:])
    for ref in plane_refs[1:]:
        total += ref[:, :half].astype(F32)
        core += unpack_core(ref[:, half:])
    core_ref[...] = pack_core(core)
    half_ref[...] = total.astype(BF16)


def add_kernel(*refs):
    *parts, sum_ref = refs
    total = parts[0][...]
    for ref in parts[1:]:
        total += ref[...].astype(F32)
    sum_ref[...] = total.astype(BF16)


def solve_mixer(core):
    rank = core.shape[0]
    gram = lax.dot_general(
        core, core, (((0,), (0,)), ((), ())), precision=lax.Precision.HIGHEST, preferred_element_type=F32
    )
    r = lax.broadcasted_iota(jnp.int32, (rank, rank), 0)
    c = lax.broadcasted_iota(jnp.int32, (rank, rank), 1)
    eye = (r == c).astype(F32)
    shift = ridge_scale * (jnp.sum(gram * eye) / rank + 1e-06)
    table = jnp.concatenate([gram + shift * eye, core.T], axis=1)
    width = table.shape[1]
    tall = 8
    tile = (tall, width)
    line = lax.broadcasted_iota(jnp.int32, tile, 0)
    tiles = [table[i : i + tall, :] for i in range(0, rank, tall)]
    for k in range(0, rank, 4):
        own, i = k // tall, k % tall
        cols = [[jnp.broadcast_to(t[:, k + j : k + j + 1], tile) for t in tiles] for j in range(4)]
        row = lambda t, j: jnp.broadcast_to(t[i + j : i + j + 1, :], tile)
        at = lambda m, j: row(cols[j][own], m)
        r0, r1, r2, r3 = [row(tiles[own], j) for j in range(4)]
        a, b, d = at(0, 0), at(1, 0), at(1, 1)
        e0, e1, f0, f1 = at(2, 0), at(2, 1), at(3, 0), at(3, 1)
        inv = 1.0 / (a * d - b * b)
        u0, u1 = (d * e0 - b * e1) * inv, (a * e1 - b * e0) * inv
        v0, v1 = (d * f0 - b * f1) * inv, (a * f1 - b * f0) * inv
        p = at(2, 2) - (e0 * u0 + e1 * u1)
        q = at(3, 2) - (e0 * v0 + e1 * v1)
        t = at(3, 3) - (f0 * v0 + f1 * v1)
        inv_late = 1.0 / (p * t - q * q)
        n0, n1 = (r0 * d - r1 * b) * inv, (r1 * a - r0 * b) * inv
        s2, s3 = r2 - (e0 * n0 + e1 * n1), r3 - (f0 * n0 + f1 * n1)
        n2, n3 = (s2 * t - s3 * q) * inv_late, (s3 * p - s2 * q) * inv_late
        n0, n1 = n0 - (u0 * n2 + v0 * n3), n1 - (u1 * n2 + v1 * n3)
        for j in range(4):
            cols[j][own] = cols[j][own] - (line == i + j).astype(F32)
        tiles = [
            x - ((c0 * n0 + c1 * n1) + (c2 * n2 + c3 * n3)) for x, c0, c1, c2, c3 in zip(tiles, *cols)
        ]
    return jnp.concatenate(tiles, axis=0)[:, rank:]


def solve_kernel(where_ref, own_half_ref, got_half_ref, *rest):
    *core_refs, left_ref = rest
    half = own_half_ref.shape[1]
    core = unpack_core(core_refs[0][...])
    for ref in core_refs[1:]:
        core += unpack_core(ref[...])
    high, low = split2(solve_mixer(core))
    side = where_ref[0]
    for k, ref in enumerate((own_half_ref, got_half_ref)):
        y1 = ref[...]
        left = dot(y1, high, ((0,), (0,))) + dot(y1, low, ((0,), (0,)))
        slot = jnp.bitwise_xor(side, k)
        left_ref[pl.ds(pl.multiple_of(slot * half, half), half), :] = left.astype(BF16)


def join_right(where_ref, right_refs, right_scr):
    share = right_refs[0].shape[1]
    for k, ref in enumerate(right_refs):
        slot = jnp.bitwise_xor(where_ref[1], k)
        right_scr[:, pl.ds(pl.multiple_of(slot * share, LANES), share)] = ref[...]


def middle_kernel(n_row, chunk, where_ref, movie_ref, vpt_ref, fpt_ref, left_ref, *rest):
    right_refs = rest[:n_row]
    own_ref, send_ref = rest[n_row : 2 + n_row]
    *y2_refs, right_scr, cur_scr, y1_scr, y2_scr = rest[2 + n_row :]
    step = pl.program_id(0)
    rows, voxels = cur_scr.shape

    @pl.when(step == 0)
    def _():
        join_right(where_ref, right_refs, right_scr)
        y2_scr[...] = jnp.zeros_like(y2_scr)

    span = pl.ds(pl.multiple_of(step * rows, rows), rows)
    left = left_ref[span, :]
    fpt = fpt_ref[...]
    cols = [slice(j, j + chunk) for j in range(0, voxels, chunk)]
    bound = jnp.asarray(cutoff, BF16)

    def sketch(c, y1):
        cur = cur_scr[:, c]
        y2_scr[:, c] += dot(fpt, cur)
        part = dot(vpt_ref[:, c], cur, ((1,), (1,)))
        return part if y1 is None else y1 + part

    y1 = None
    ahead = dot(left, right_scr[:, cols[0]])
    for j, c in enumerate(cols):
        low = ahead.astype(BF16)
        if j + 1 < len(cols):
            ahead = dot(left, right_scr[:, cols[j + 1]])
        cur_scr[:, c] = low + jnp.clip(movie_ref[span, c] - low, -bound, bound)
        if j > 0:
            y1 = sketch(cols[j - 1], y1)
    y1_scr[:, span] = sketch(cols[-1], y1)

    @pl.when(step == pl.num_programs(0) - 1)
    def _():
        finish_sketch(where_ref, y1_scr, y2_scr, vpt_ref, own_ref, send_ref, y2_refs)


def last_kernel(n_row, chunk, where_ref, movie_ref, left_ref, *rest):
    right_refs = rest[:n_row]
    low_ref, sparse_ref, right_scr = rest[n_row:]
    step = pl.program_id(0)
    rows, voxels = low_ref.shape

    @pl.when(step == 0)
    def _():
        join_right(where_ref, right_refs, right_scr)

    span = pl.ds(pl.multiple_of(step * rows, rows), rows)
    left = left_ref[span, :]
    cols = [slice(j, j + chunk) for j in range(0, voxels, chunk)]
    ahead = dot(left, right_scr[:, cols[0]])
    for j, c in enumerate(cols):
        low = ahead
        if j + 1 < len(cols):
            ahead = dot(left, right_scr[:, cols[j + 1]])
        low_ref[:, c] = low.astype(BF16)
        gap = movie_ref[span, c].astype(F32) - low
        sparse_ref[:, c] = (gap - jnp.clip(gap, -cutoff, cutoff)).astype(BF16)


def block_rows(rows, width):
    return pl.BlockSpec((rows, width), lambda i, *_: (i, 0))


def block_cols(rank, rows):
    return pl.BlockSpec((rank, rows), lambda i, *_: (0, i))


def size_of(arrays):
    return sum(a.size * a.dtype.itemsize for a in arrays)


def vmem_call(kernel, outs, args, flops=1e6, where=None):
    resident = pl.BlockSpec(memory_space=pltpu.VMEM)
    return pl.pallas_call(
        kernel,
        out_shape=outs,
        in_specs=([] if where is None else [pl.BlockSpec(memory_space=pltpu.SMEM)]) + [resident] * len(args),
        out_specs=[resident] * len(outs),
        compiler_params=pltpu.CompilerParams(vmem_limit_bytes=8 * 1024 * 1024),
        cost_estimate=pl.CostEstimate(flops=int(flops), bytes_accessed=size_of([*args, *outs]), transcendentals=0),
    )(*([] if where is None else [where]), *args)


def exchange(x, axis, k):
    size = lax.axis_size(axis)
    return lax.ppermute(x, axis, [(i, i ^ k) for i in range(size)])


def on_device(movie, voxel_probe, frame_probe):
    frames, voxels = movie.shape
    rank = voxel_probe.shape[1]
    n_vox, n_row = lax.axis_size("vox"), lax.axis_size("frm")
    half, share = frames // 2, voxels // n_row
    width = half + 2 * rank
    rows = min(512, frames)
    last_rows = min(256, frames)
    chunk = min(256, voxels)
    where = jnp.stack([lax.axis_index("vox") % 2, lax.axis_index("frm")]).astype(jnp.int32)
    vpt, fpt = voxel_probe.T, frame_probe.T

    resident = pl.BlockSpec(memory_space=pltpu.VMEM)
    sketch_shapes = [
        jax.ShapeDtypeStruct((rank, width), F32),
        jax.ShapeDtypeStruct((rank, width), BF16),
        jax.ShapeDtypeStruct((rank, share), F32),
    ] + [jax.ShapeDtypeStruct((rank, share), BF16)] * (n_row - 1)
    sketch_specs = [resident] * len(sketch_shapes)
    sums = [pltpu.VMEM((rank, frames), F32), pltpu.VMEM((rank, voxels), F32)]
    right = pltpu.VMEM((rank, voxels), BF16)
    probe_specs = [resident, block_cols(rank, rows)]
    side_specs = [resident] * (1 + n_row)

    def run(kernel, steps, in_specs, out_specs, out_shape, scratch, passes, args, limit=20 * 1024 * 1024):
        return pl.pallas_call(
            kernel,
            grid_spec=pltpu.PrefetchScalarGridSpec(
                num_scalar_prefetch=1,
                grid=(steps,),
                in_specs=in_specs,
                out_specs=out_specs,
                scratch_shapes=scratch,
            ),
            out_shape=out_shape,
            compiler_params=pltpu.CompilerParams(
                dimension_semantics=("arbitrary",), vmem_limit_bytes=limit
            ),
            cost_estimate=pl.CostEstimate(
                flops=2 * passes * frames * voxels * rank, bytes_accessed=2 * frames * voxels, transcendentals=0
            ),
        )(where, *args)

    def share_sketch(own, send, *y2_parts):
        got = exchange(send, "vox", 1)
        (msg,) = vmem_call(pair_kernel, [jax.ShapeDtypeStruct((rank, width), BF16)], [own, got])
        plane = [msg] + [exchange(msg, "vox", 2 * k) for k in range(1, n_vox // 2)]
        parts = [y2_parts[0]] + [exchange(y2_parts[k], "frm", k) for k in range(1, n_row)]
        own_half, core = vmem_call(
            plane_kernel,
            [jax.ShapeDtypeStruct((rank, half), BF16), jax.ShapeDtypeStruct((rank, 2 * rank), BF16)],
            plane,
        )
        cores = [core] + [exchange(core, "frm", k) for k in range(1, n_row)]
        got_half = exchange(own_half, "vox", 1)
        (mine,) = vmem_call(add_kernel, [jax.ShapeDtypeStruct((rank, share), BF16)], parts)
        rights = [mine] + [exchange(mine, "frm", k) for k in range(1, n_row)]
        (left,) = vmem_call(
            solve_kernel,
            [jax.ShapeDtypeStruct((frames, rank), BF16)],
            [own_half, got_half, *cores],
            flops=5e9,
            where=where,
        )
        return [left, *rights]

    sketch = run(
        first_kernel,
        frames // rows,
        [block_rows(rows, voxels), pl.BlockSpec((rank, voxels), lambda i, *_: (0, 0)), block_cols(rank, rows)],
        sketch_specs,
        sketch_shapes,
        sums,
        2,
        tuple(pltpu.with_memory_space_constraint(x, pltpu.HBM) for x in (movie, vpt, fpt)),
        limit=44 * 1024 * 1024,
    )
    sides = share_sketch(*sketch)
    for _ in range(1, ITERS):
        sketch = run(
            functools.partial(middle_kernel, n_row, chunk),
            frames // rows,
            [resident] + probe_specs + side_specs,
            sketch_specs,
            sketch_shapes,
            [right, pltpu.VMEM((rows, voxels), BF16)] + sums,
            3,
            (movie, vpt, fpt, *sides),
        )
        sides = share_sketch(*sketch)
    out = jax.ShapeDtypeStruct((frames, voxels), BF16)
    return tuple(
        run(
            functools.partial(last_kernel, n_row, chunk),
            frames // last_rows,
            [resident] + side_specs,
            [block_rows(last_rows, voxels)] * 2,
            [out, out],
            [right],
            1,
            (movie, *sides),
        )
    )


def solution(mesh):
    return jax.shard_map(
        on_device,
        mesh=mesh,
        in_specs=(P("frm", "vox"), P("vox", None), P("frm", None)),
        out_specs=(P("frm", "vox"), P("frm", "vox")),
        check_vma=False,
    )
```

```python
import functools

import jax
import jax.numpy as jnp
from jax import lax
from jax.experimental import pallas as pl
from jax.experimental.pallas import tpu as pltpu
from jax.sharding import PartitionSpec as P

ITERS = 2
cutoff = 1.0
ridge_scale = 0.1


F32 = jnp.float32
BF16 = jnp.bfloat16
LANES = 128


def dot(a, b, contract=((1,), (0,))):
    return lax.dot_general(a, b, (contract, ((), ())), preferred_element_type=F32)


def split2(x):
    high = x.astype(BF16)
    return high, (x - high.astype(F32)).astype(BF16)


def pack_core(core):
    high, low = split2(core)
    return jnp.concatenate([high, low], axis=1)


def unpack_core(packed):
    rank = packed.shape[0]
    wide = packed.astype(F32)
    return wide[:, :rank] + wide[:, rank:]


def finish_sketch(where_ref, y1_scr, y2_scr, vpt_ref, own_ref, send_ref, y2_refs):
    rank, frames = y1_scr.shape
    half = frames // 2
    peers = len(y2_refs)
    share = y2_scr.shape[1] // peers
    y2 = y2_scr[...]
    high, rest = split2(y2)
    low = (y2 - high.astype(F32) - rest.astype(F32)).astype(BF16)
    vp = vpt_ref[...]
    parts = dot(jnp.concatenate([high, rest, low], axis=0), vp, ((1,), (1,)))
    core = parts[:rank] + parts[rank : 2 * rank] + parts[2 * rank :]
    side = where_ref[0]
    row = where_ref[1]
    own_ref[:, :half] = y1_scr[:, pl.ds(pl.multiple_of(side * half, LANES), half)]
    own_ref[:, half : half + 2 * rank] = jnp.concatenate([core, jnp.zeros_like(core)], axis=1)
    other = y1_scr[:, pl.ds(pl.multiple_of((1 - side) * half, LANES), half)]
    send_ref[:, :half] = other.astype(BF16)
    send_ref[:, half : half + 2 * rank] = pack_core(core)
    for k in range(peers):
        slot = jnp.bitwise_xor(row, k)
        part = y2_scr[:, pl.ds(pl.multiple_of(slot * share, LANES), share)]
        y2_refs[k][...] = part.astype(y2_refs[k].dtype)


def first_kernel(where_ref, movie_ref, vpt_ref, fpt_ref, own_ref, send_ref, *rest):
    *y2_refs, y1_scr, y2_scr = rest
    step = pl.program_id(0)
    rows = movie_ref.shape[0]

    @pl.when(step == 0)
    def _():
        y2_scr[...] = jnp.zeros_like(y2_scr)

    cur = movie_ref[...]
    y2_scr[...] += dot(fpt_ref[...], cur)
    y1_scr[:, pl.ds(pl.multiple_of(step * rows, rows), rows)] = dot(vpt_ref[...], cur, ((1,), (1,)))

    @pl.when(step == pl.num_programs(0) - 1)
    def _():
        finish_sketch(where_ref, y1_scr, y2_scr, vpt_ref, own_ref, send_ref, y2_refs)


def pair_kernel(own_ref, got_ref, msg_ref):
    rank, width = own_ref.shape
    half = width - 2 * rank
    msg_ref[:, :half] = (own_ref[:, :half] + got_ref[:, :half].astype(F32)).astype(BF16)
    core = own_ref[:, half:][:, :rank] + unpack_core(got_ref[:, half:])
    msg_ref[:, half:] = pack_core(core)


def plane_kernel(*refs):
    *plane_refs, half_ref, core_ref = refs
    half = half_ref.shape[1]
    total = plane_refs[0][:, :half].astype(F32)
    core = unpack_core(plane_refs[0][:, half:])
    for ref in plane_refs[1:]:
        total += ref[:, :half].astype(F32)
        core += unpack_core(ref[:, half:])
    core_ref[...] = pack_core(core)
    half_ref[...] = total.astype(BF16)


def add_kernel(*refs):
    *parts, sum_ref = refs
    total = parts[0][...]
    for ref in parts[1:]:
        total += ref[...].astype(F32)
    sum_ref[...] = total.astype(BF16)


def solve_mixer(core):
    rank = core.shape[0]
    gram = lax.dot_general(
        core, core, (((0,), (0,)), ((), ())), precision=lax.Precision.HIGHEST, preferred_element_type=F32
    )
    r = lax.broadcasted_iota(jnp.int32, (rank, rank), 0)
    c = lax.broadcasted_iota(jnp.int32, (rank, rank), 1)
    eye = (r == c).astype(F32)
    shift = ridge_scale * (jnp.sum(gram * eye) / rank + 1e-06)
    table = jnp.concatenate([gram + shift * eye, core.T], axis=1)
    width = table.shape[1]
    tall = 8
    tile = (tall, width)
    line = lax.broadcasted_iota(jnp.int32, tile, 0)
    tiles = [table[i : i + tall, :] for i in range(0, rank, tall)]
    for k in range(0, rank, 4):
        own, i = k // tall, k % tall
        cols = [[jnp.broadcast_to(t[:, k + j : k + j + 1], tile) for t in tiles] for j in range(4)]
        row = lambda t, j: jnp.broadcast_to(t[i + j : i + j + 1, :], tile)
        at = lambda m, j: row(cols[j][own], m)
        r0, r1, r2, r3 = [row(tiles[own], j) for j in range(4)]
        a, b, d = at(0, 0), at(1, 0), at(1, 1)
        e0, e1, f0, f1 = at(2, 0), at(2, 1), at(3, 0), at(3, 1)
        inv = 1.0 / (a * d - b * b)
        u0, u1 = (d * e0 - b * e1) * inv, (a * e1 - b * e0) * inv
        v0, v1 = (d * f0 - b * f1) * inv, (a * f1 - b * f0) * inv
        p = at(2, 2) - (e0 * u0 + e1 * u1)
        q = at(3, 2) - (e0 * v0 + e1 * v1)
        t = at(3, 3) - (f0 * v0 + f1 * v1)
        inv_late = 1.0 / (p * t - q * q)
        n0, n1 = (r0 * d - r1 * b) * inv, (r1 * a - r0 * b) * inv
        s2, s3 = r2 - (e0 * n0 + e1 * n1), r3 - (f0 * n0 + f1 * n1)
        n2, n3 = (s2 * t - s3 * q) * inv_late, (s3 * p - s2 * q) * inv_late
        n0, n1 = n0 - (u0 * n2 + v0 * n3), n1 - (u1 * n2 + v1 * n3)
        for j in range(4):
            cols[j][own] = cols[j][own] - (line == i + j).astype(F32)
        tiles = [
            x - ((c0 * n0 + c1 * n1) + (c2 * n2 + c3 * n3)) for x, c0, c1, c2, c3 in zip(tiles, *cols)
        ]
    return jnp.concatenate(tiles, axis=0)[:, rank:]


def solve_kernel(where_ref, own_half_ref, got_half_ref, *rest):
    *core_refs, left_ref = rest
    half = own_half_ref.shape[1]
    core = unpack_core(core_refs[0][...])
    for ref in core_refs[1:]:
        core += unpack_core(ref[...])
    high, low = split2(solve_mixer(core))
    side = where_ref[0]
    for k, ref in enumerate((own_half_ref, got_half_ref)):
        y1 = ref[...]
        left = dot(y1, high, ((0,), (0,))) + dot(y1, low, ((0,), (0,)))
        slot = jnp.bitwise_xor(side, k)
        left_ref[pl.ds(pl.multiple_of(slot * half, half), half), :] = left.astype(BF16)


def join_right(where_ref, right_refs, right_scr):
    share = right_refs[0].shape[1]
    for k, ref in enumerate(right_refs):
        slot = jnp.bitwise_xor(where_ref[1], k)
        right_scr[:, pl.ds(pl.multiple_of(slot * share, LANES), share)] = ref[...]


def middle_kernel(n_row, chunk, where_ref, movie_ref, vpt_ref, fpt_ref, left_ref, *rest):
    right_refs = rest[:n_row]
    own_ref, send_ref = rest[n_row : 2 + n_row]
    *y2_refs, right_scr, cur_scr, y1_scr, y2_scr = rest[2 + n_row :]
    step = pl.program_id(0)
    rows, voxels = cur_scr.shape

    @pl.when(step == 0)
    def _():
        join_right(where_ref, right_refs, right_scr)
        y2_scr[...] = jnp.zeros_like(y2_scr)

    span = pl.ds(pl.multiple_of(step * rows, rows), rows)
    left = left_ref[span, :]
    fpt = fpt_ref[...]
    cols = [slice(j, j + chunk) for j in range(0, voxels, chunk)]
    bound = jnp.asarray(cutoff, BF16)

    def sketch(c, y1):
        cur = cur_scr[:, c]
        y2_scr[:, c] += dot(fpt, cur)
        part = dot(vpt_ref[:, c], cur, ((1,), (1,)))
        return part if y1 is None else y1 + part

    y1 = None
    ahead = dot(left, right_scr[:, cols[0]])
    for j, c in enumerate(cols):
        low = ahead.astype(BF16)
        if j + 1 < len(cols):
            ahead = dot(left, right_scr[:, cols[j + 1]])
        cur_scr[:, c] = low + jnp.clip(movie_ref[span, c] - low, -bound, bound)
        if j > 0:
            y1 = sketch(cols[j - 1], y1)
    y1_scr[:, span] = sketch(cols[-1], y1)

    @pl.when(step == pl.num_programs(0) - 1)
    def _():
        finish_sketch(where_ref, y1_scr, y2_scr, vpt_ref, own_ref, send_ref, y2_refs)


def last_kernel(n_row, chunk, where_ref, movie_ref, left_ref, *rest):
    right_refs = rest[:n_row]
    low_ref, sparse_ref, right_scr = rest[n_row:]
    step = pl.program_id(0)
    rows, voxels = low_ref.shape

    @pl.when(step == 0)
    def _():
        join_right(where_ref, right_refs, right_scr)

    span = pl.ds(pl.multiple_of(step * rows, rows), rows)
    left = left_ref[span, :]
    cols = [slice(j, j + chunk) for j in range(0, voxels, chunk)]
    ahead = dot(left, right_scr[:, cols[0]])
    for j, c in enumerate(cols):
        low = ahead
        if j + 1 < len(cols):
            ahead = dot(left, right_scr[:, cols[j + 1]])
        low_ref[:, c] = low.astype(BF16)
        gap = movie_ref[span, c].astype(F32) - low
        sparse_ref[:, c] = (gap - jnp.clip(gap, -cutoff, cutoff)).astype(BF16)


def block_rows(rows, width):
    return pl.BlockSpec((rows, width), lambda i, *_: (i, 0))


def block_cols(rank, rows):
    return pl.BlockSpec((rank, rows), lambda i, *_: (0, i))


def size_of(arrays):
    return sum(a.size * a.dtype.itemsize for a in arrays)


def vmem_call(kernel, outs, args, flops=1e6, where=None):
    resident = pl.BlockSpec(memory_space=pltpu.VMEM)
    return pl.pallas_call(
        kernel,
        out_shape=outs,
        in_specs=([] if where is None else [pl.BlockSpec(memory_space=pltpu.SMEM)]) + [resident] * len(args),
        out_specs=[resident] * len(outs),
        compiler_params=pltpu.CompilerParams(vmem_limit_bytes=8 * 1024 * 1024),
        cost_estimate=pl.CostEstimate(flops=int(flops), bytes_accessed=size_of([*args, *outs]), transcendentals=0),
    )(*([] if where is None else [where]), *args)


def exchange(x, axis, k):
    size = lax.axis_size(axis)
    return lax.ppermute(x, axis, [(i, i ^ k) for i in range(size)])


def on_device(movie, voxel_probe, frame_probe):
    frames, voxels = movie.shape
    rank = voxel_probe.shape[1]
    n_vox, n_row = lax.axis_size("vox"), lax.axis_size("frm")
    half, share = frames // 2, voxels // n_row
    width = half + 2 * rank
    rows = min(512, frames)
    mid_rows = min(1024, frames)
    last_rows = min(512, frames)
    chunk = min(256, voxels)
    where = jnp.stack([lax.axis_index("vox") % 2, lax.axis_index("frm")]).astype(jnp.int32)
    vpt, fpt = voxel_probe.T, frame_probe.T

    resident = pl.BlockSpec(memory_space=pltpu.VMEM)
    sketch_shapes = [
        jax.ShapeDtypeStruct((rank, width), F32),
        jax.ShapeDtypeStruct((rank, width), BF16),
        jax.ShapeDtypeStruct((rank, share), F32),
    ] + [jax.ShapeDtypeStruct((rank, share), BF16)] * (n_row - 1)
    sketch_specs = [resident] * len(sketch_shapes)
    sums = [pltpu.VMEM((rank, frames), F32), pltpu.VMEM((rank, voxels), F32)]
    right = pltpu.VMEM((rank, voxels), BF16)
    probe_specs = [resident, block_cols(rank, rows)]
    side_specs = [resident] * (1 + n_row)

    def run(kernel, steps, in_specs, out_specs, out_shape, scratch, passes, args, limit=20 * 1024 * 1024):
        return pl.pallas_call(
            kernel,
            grid_spec=pltpu.PrefetchScalarGridSpec(
                num_scalar_prefetch=1,
                grid=(steps,),
                in_specs=in_specs,
                out_specs=out_specs,
                scratch_shapes=scratch,
            ),
            out_shape=out_shape,
            compiler_params=pltpu.CompilerParams(
                dimension_semantics=("arbitrary",), vmem_limit_bytes=limit
            ),
            cost_estimate=pl.CostEstimate(
                flops=2 * passes * frames * voxels * rank, bytes_accessed=2 * frames * voxels, transcendentals=0
            ),
        )(where, *args)

    def share_sketch(own, send, *y2_parts):
        got = exchange(send, "vox", 1)
        (msg,) = vmem_call(pair_kernel, [jax.ShapeDtypeStruct((rank, width), BF16)], [own, got])
        plane = [msg] + [exchange(msg, "vox", 2 * k) for k in range(1, n_vox // 2)]
        parts = [y2_parts[0]] + [exchange(y2_parts[k], "frm", k) for k in range(1, n_row)]
        own_half, core = vmem_call(
            plane_kernel,
            [jax.ShapeDtypeStruct((rank, half), BF16), jax.ShapeDtypeStruct((rank, 2 * rank), BF16)],
            plane,
        )
        cores = [core] + [exchange(core, "frm", k) for k in range(1, n_row)]
        got_half = exchange(own_half, "vox", 1)
        (mine,) = vmem_call(add_kernel, [jax.ShapeDtypeStruct((rank, share), BF16)], parts)
        rights = [mine] + [exchange(mine, "frm", k) for k in range(1, n_row)]
        (left,) = vmem_call(
            solve_kernel,
            [jax.ShapeDtypeStruct((frames, rank), BF16)],
            [own_half, got_half, *cores],
            flops=5e9,
            where=where,
        )
        return [left, *rights]

    sketch = run(
        first_kernel,
        frames // rows,
        [block_rows(rows, voxels), pl.BlockSpec((rank, voxels), lambda i, *_: (0, 0)), block_cols(rank, rows)],
        sketch_specs,
        sketch_shapes,
        sums,
        2,
        tuple(pltpu.with_memory_space_constraint(x, pltpu.HBM) for x in (movie, vpt, fpt)),
        limit=44 * 1024 * 1024,
    )
    sides = share_sketch(*sketch)
    for _ in range(1, ITERS):
        sketch = run(
            functools.partial(middle_kernel, n_row, chunk),
            frames // mid_rows,
            [resident, resident, block_cols(rank, mid_rows)] + side_specs,
            sketch_specs,
            sketch_shapes,
            [right, pltpu.VMEM((mid_rows, voxels), BF16)] + sums,
            3,
            (movie, vpt, fpt, *sides),
        )
        sides = share_sketch(*sketch)
    out = jax.ShapeDtypeStruct((frames, voxels), BF16)
    return tuple(
        run(
            functools.partial(last_kernel, n_row, 256),
            frames // last_rows,
            [resident] + side_specs,
            [block_rows(last_rows, voxels)] * 2,
            [out, out],
            [right],
            1,
            (movie, *sides),
        )
    )


def solution(mesh):
    return jax.shard_map(
        on_device,
        mesh=mesh,
        in_specs=(P("frm", "vox"), P("vox", None), P("frm", None)),
        out_specs=(P("frm", "vox"), P("frm", "vox")),
        check_vma=False,
    )
```

```python
import functools

import jax
import jax.numpy as jnp
from jax import lax
from jax.experimental import pallas as pl
from jax.experimental.pallas import tpu as pltpu
from jax.sharding import PartitionSpec as P

ITERS = 2
cutoff = 1.0
ridge_scale = 0.1


F32 = jnp.float32
BF16 = jnp.bfloat16
LANES = 128


def dot(a, b, contract=((1,), (0,))):
    return lax.dot_general(a, b, (contract, ((), ())), preferred_element_type=F32)


def split2(x):
    high = x.astype(BF16)
    return high, (x - high.astype(F32)).astype(BF16)


def pack_core(core):
    high, low = split2(core)
    return jnp.concatenate([high, low], axis=1)


def unpack_core(packed):
    rank = packed.shape[0]
    wide = packed.astype(F32)
    return wide[:, :rank] + wide[:, rank:]


def finish_sketch(where_ref, y1_scr, y2_scr, vpt_ref, own_ref, send_ref, y2_refs):
    rank, frames = y1_scr.shape
    half = frames // 2
    peers = len(y2_refs)
    share = y2_scr.shape[1] // peers
    y2 = y2_scr[...]
    high, rest = split2(y2)
    low = (y2 - high.astype(F32) - rest.astype(F32)).astype(BF16)
    vp = vpt_ref[...]
    parts = dot(jnp.concatenate([high, rest, low], axis=0), vp, ((1,), (1,)))
    core = parts[:rank] + parts[rank : 2 * rank] + parts[2 * rank :]
    side = where_ref[0]
    row = where_ref[1]
    own_ref[:, :half] = y1_scr[:, pl.ds(pl.multiple_of(side * half, LANES), half)]
    own_ref[:, half : half + 2 * rank] = jnp.concatenate([core, jnp.zeros_like(core)], axis=1)
    other = y1_scr[:, pl.ds(pl.multiple_of((1 - side) * half, LANES), half)]
    send_ref[:, :half] = other.astype(BF16)
    send_ref[:, half : half + 2 * rank] = pack_core(core)
    for k in range(peers):
        slot = jnp.bitwise_xor(row, k)
        part = y2_scr[:, pl.ds(pl.multiple_of(slot * share, LANES), share)]
        y2_refs[k][...] = part.astype(y2_refs[k].dtype)


def first_kernel(blocks, where_ref, movie_ref, vpt_hbm, fpt_hbm, own_ref, send_ref, *rest):
    *y2_refs, held, vpt_ref, fpt_ref, y1_scr, y2_scr, sems = rest
    spans = [slice(start, stop) for start, stop in zip(blocks, blocks[1:])]
    copies = [
        pltpu.make_async_copy(movie_ref.at[span, :], held.at[span, :], sems.at[i]) for i, span in enumerate(spans)
    ]
    probes = [
        pltpu.make_async_copy(fpt_hbm, fpt_ref, sems.at[len(spans)]),
        pltpu.make_async_copy(vpt_hbm, vpt_ref, sems.at[len(spans) + 1]),
    ]
    for copy in [copies[0], *probes, *copies[1:]]:
        copy.start()
    for copy in probes:
        copy.wait()
    for i, span in enumerate(spans):
        copies[i].wait()
        cur = held[span, :]
        part = dot(fpt_ref[:, span], cur)
        y2_scr[...] = part if i == 0 else y2_scr[...] + part
        y1_scr[:, span] = dot(vpt_ref[...], cur, ((1,), (1,)))
    finish_sketch(where_ref, y1_scr, y2_scr, vpt_ref, own_ref, send_ref, y2_refs)


def pair_kernel(own_ref, got_ref, msg_ref):
    rank, width = own_ref.shape
    half = width - 2 * rank
    msg_ref[:, :half] = (own_ref[:, :half] + got_ref[:, :half].astype(F32)).astype(BF16)
    core = own_ref[:, half:][:, :rank] + unpack_core(got_ref[:, half:])
    msg_ref[:, half:] = pack_core(core)


def plane_kernel(*refs):
    *plane_refs, half_ref, core_ref = refs
    half = half_ref.shape[1]
    total = plane_refs[0][:, :half].astype(F32)
    core = unpack_core(plane_refs[0][:, half:])
    for ref in plane_refs[1:]:
        total += ref[:, :half].astype(F32)
        core += unpack_core(ref[:, half:])
    core_ref[...] = pack_core(core)
    half_ref[...] = total.astype(BF16)


def add_kernel(*refs):
    *parts, sum_ref = refs
    total = parts[0][...]
    for ref in parts[1:]:
        total += ref[...].astype(F32)
    sum_ref[...] = total.astype(BF16)


def solve_mixer(core):
    rank = core.shape[0]
    gram = lax.dot_general(
        core, core, (((0,), (0,)), ((), ())), precision=lax.Precision.HIGHEST, preferred_element_type=F32
    )
    r = lax.broadcasted_iota(jnp.int32, (rank, rank), 0)
    c = lax.broadcasted_iota(jnp.int32, (rank, rank), 1)
    eye = (r == c).astype(F32)
    shift = ridge_scale * (jnp.sum(gram * eye) / rank + 1e-06)
    table = jnp.concatenate([gram + shift * eye, core.T], axis=1)
    width = table.shape[1]
    tall = 8
    tile = (tall, width)
    line = lax.broadcasted_iota(jnp.int32, tile, 0)
    tiles = [table[i : i + tall, :] for i in range(0, rank, tall)]
    for k in range(0, rank, 4):
        own, i = k // tall, k % tall
        cols = [[jnp.broadcast_to(t[:, k + j : k + j + 1], tile) for t in tiles] for j in range(4)]
        row = lambda t, j: jnp.broadcast_to(t[i + j : i + j + 1, :], tile)
        at = lambda m, j: row(cols[j][own], m)
        r0, r1, r2, r3 = [row(tiles[own], j) for j in range(4)]
        a, b, d = at(0, 0), at(1, 0), at(1, 1)
        e0, e1, f0, f1 = at(2, 0), at(2, 1), at(3, 0), at(3, 1)
        inv = 1.0 / (a * d - b * b)
        u0, u1 = (d * e0 - b * e1) * inv, (a * e1 - b * e0) * inv
        v0, v1 = (d * f0 - b * f1) * inv, (a * f1 - b * f0) * inv
        p = at(2, 2) - (e0 * u0 + e1 * u1)
        q = at(3, 2) - (e0 * v0 + e1 * v1)
        t = at(3, 3) - (f0 * v0 + f1 * v1)
        inv_late = 1.0 / (p * t - q * q)
        n0, n1 = (r0 * d - r1 * b) * inv, (r1 * a - r0 * b) * inv
        s2, s3 = r2 - (e0 * n0 + e1 * n1), r3 - (f0 * n0 + f1 * n1)
        n2, n3 = (s2 * t - s3 * q) * inv_late, (s3 * p - s2 * q) * inv_late
        n0, n1 = n0 - (u0 * n2 + v0 * n3), n1 - (u1 * n2 + v1 * n3)
        for j in range(4):
            cols[j][own] = cols[j][own] - (line == i + j).astype(F32)
        tiles = [
            x - ((c0 * n0 + c1 * n1) + (c2 * n2 + c3 * n3)) for x, c0, c1, c2, c3 in zip(tiles, *cols)
        ]
    return jnp.concatenate(tiles, axis=0)[:, rank:]


def solve_kernel(where_ref, own_half_ref, got_half_ref, *rest):
    *core_refs, left_ref = rest
    half = own_half_ref.shape[1]
    core = unpack_core(core_refs[0][...])
    for ref in core_refs[1:]:
        core += unpack_core(ref[...])
    high, low = split2(solve_mixer(core))
    side = where_ref[0]
    for k, ref in enumerate((own_half_ref, got_half_ref)):
        y1 = ref[...]
        left = dot(y1, high, ((0,), (0,))) + dot(y1, low, ((0,), (0,)))
        slot = jnp.bitwise_xor(side, k)
        left_ref[pl.ds(pl.multiple_of(slot * half, half), half), :] = left.astype(BF16)


def join_right(where_ref, right_refs, right_scr):
    share = right_refs[0].shape[1]
    for k, ref in enumerate(right_refs):
        slot = jnp.bitwise_xor(where_ref[1], k)
        right_scr[:, pl.ds(pl.multiple_of(slot * share, LANES), share)] = ref[...]


def middle_kernel(n_row, chunk, where_ref, movie_ref, vpt_ref, fpt_ref, left_ref, *rest):
    right_refs = rest[:n_row]
    own_ref, send_ref = rest[n_row : 2 + n_row]
    *y2_refs, right_scr, cur_scr, y1_scr, y2_scr = rest[2 + n_row :]
    step = pl.program_id(0)
    rows, voxels = cur_scr.shape

    @pl.when(step == 0)
    def _():
        join_right(where_ref, right_refs, right_scr)
        y2_scr[...] = jnp.zeros_like(y2_scr)

    span = pl.ds(pl.multiple_of(step * rows, rows), rows)
    left = left_ref[span, :]
    fpt = fpt_ref[...]
    cols = [slice(j, j + chunk) for j in range(0, voxels, chunk)]
    bound = jnp.asarray(cutoff, BF16)

    def sketch(c, y1):
        cur = cur_scr[:, c]
        y2_scr[:, c] += dot(fpt, cur)
        part = dot(vpt_ref[:, c], cur, ((1,), (1,)))
        return part if y1 is None else y1 + part

    y1 = None
    ahead = dot(left, right_scr[:, cols[0]])
    for j, c in enumerate(cols):
        low = ahead.astype(BF16)
        if j + 1 < len(cols):
            ahead = dot(left, right_scr[:, cols[j + 1]])
        cur_scr[:, c] = low + jnp.clip(movie_ref[span, c] - low, -bound, bound)
        if j > 0:
            y1 = sketch(cols[j - 1], y1)
    y1_scr[:, span] = sketch(cols[-1], y1)

    @pl.when(step == pl.num_programs(0) - 1)
    def _():
        finish_sketch(where_ref, y1_scr, y2_scr, vpt_ref, own_ref, send_ref, y2_refs)


def last_kernel(n_row, chunk, blocks, where_ref, movie_ref, left_ref, *rest):
    right_refs = rest[:n_row]
    low_ref, sparse_ref, right_scr, low_scr, sparse_scr, sems = rest[n_row:]
    voxels = low_scr.shape[1]
    join_right(where_ref, right_refs, right_scr)
    cols = [slice(j, j + chunk) for j in range(0, voxels, chunk)]
    copies = []
    for i, span in enumerate(slice(start, stop) for start, stop in zip(blocks, blocks[1:])):
        left = left_ref[span, :]
        ahead = dot(left, right_scr[:, cols[0]])
        for j, c in enumerate(cols):
            low = ahead
            if j + 1 < len(cols):
                ahead = dot(left, right_scr[:, cols[j + 1]])
            low_scr[span, c] = low.astype(BF16)
            gap = movie_ref[span, c].astype(F32) - low
            sparse_scr[span, c] = (gap - jnp.clip(gap, -cutoff, cutoff)).astype(BF16)
        for k, (scr, ref) in enumerate(((low_scr, low_ref), (sparse_scr, sparse_ref))):
            copies.append(pltpu.make_async_copy(scr.at[span, :], ref.at[span, :], sems.at[i, k]))
            copies[-1].start()
    for copy in copies:
        copy.wait()


def block_cols(rank, rows):
    return pl.BlockSpec((rank, rows), lambda i, *_: (0, i))


def size_of(arrays):
    return sum(a.size * a.dtype.itemsize for a in arrays)


def vmem_call(kernel, outs, args, flops=1e6, where=None):
    resident = pl.BlockSpec(memory_space=pltpu.VMEM)
    return pl.pallas_call(
        kernel,
        out_shape=outs,
        in_specs=([] if where is None else [pl.BlockSpec(memory_space=pltpu.SMEM)]) + [resident] * len(args),
        out_specs=[resident] * len(outs),
        compiler_params=pltpu.CompilerParams(vmem_limit_bytes=8 * 1024 * 1024),
        cost_estimate=pl.CostEstimate(flops=int(flops), bytes_accessed=size_of([*args, *outs]), transcendentals=0),
    )(*([] if where is None else [where]), *args)


def exchange(x, axis, k):
    size = lax.axis_size(axis)
    return lax.ppermute(x, axis, [(i, i ^ k) for i in range(size)])


def on_device(movie, voxel_probe, frame_probe):
    frames, voxels = movie.shape
    rank = voxel_probe.shape[1]
    n_vox, n_row = lax.axis_size("vox"), lax.axis_size("frm")
    half, share = frames // 2, voxels // n_row
    width = half + 2 * rank
    rows = min(512, frames)
    mid_rows = min(1024, frames)
    chunk = min(256, voxels)
    where = jnp.stack([lax.axis_index("vox") % 2, lax.axis_index("frm")]).astype(jnp.int32)
    vpt, fpt = voxel_probe.T, frame_probe.T

    resident = pl.BlockSpec(memory_space=pltpu.VMEM)
    sketch_shapes = [
        jax.ShapeDtypeStruct((rank, width), F32),
        jax.ShapeDtypeStruct((rank, width), BF16),
        jax.ShapeDtypeStruct((rank, share), F32),
    ] + [jax.ShapeDtypeStruct((rank, share), BF16)] * (n_row - 1)
    sketch_specs = [resident] * len(sketch_shapes)
    sums = [pltpu.VMEM((rank, frames), F32), pltpu.VMEM((rank, voxels), F32)]
    right = pltpu.VMEM((rank, voxels), BF16)
    probe_specs = [resident, block_cols(rank, rows)]
    side_specs = [resident] * (1 + n_row)

    def run(kernel, steps, in_specs, out_specs, out_shape, scratch, passes, args, limit=20 * 1024 * 1024):
        return pl.pallas_call(
            kernel,
            grid_spec=pltpu.PrefetchScalarGridSpec(
                num_scalar_prefetch=1,
                grid=(steps,),
                in_specs=in_specs,
                out_specs=out_specs,
                scratch_shapes=scratch,
            ),
            out_shape=out_shape,
            compiler_params=pltpu.CompilerParams(
                dimension_semantics=("arbitrary",), vmem_limit_bytes=limit
            ),
            cost_estimate=pl.CostEstimate(
                flops=2 * passes * frames * voxels * rank, bytes_accessed=2 * frames * voxels, transcendentals=0
            ),
        )(where, *args)

    def share_sketch(own, send, *y2_parts):
        got = exchange(send, "vox", 1)
        (msg,) = vmem_call(pair_kernel, [jax.ShapeDtypeStruct((rank, width), BF16)], [own, got])
        plane = [msg] + [exchange(msg, "vox", 2 * k) for k in range(1, n_vox // 2)]
        parts = [y2_parts[0]] + [exchange(y2_parts[k], "frm", k) for k in range(1, n_row)]
        own_half, core = vmem_call(
            plane_kernel,
            [jax.ShapeDtypeStruct((rank, half), BF16), jax.ShapeDtypeStruct((rank, 2 * rank), BF16)],
            plane,
        )
        cores = [core] + [exchange(core, "frm", k) for k in range(1, n_row)]
        got_half = exchange(own_half, "vox", 1)
        (mine,) = vmem_call(add_kernel, [jax.ShapeDtypeStruct((rank, share), BF16)], parts)
        rights = [mine] + [exchange(mine, "frm", k) for k in range(1, n_row)]
        (left,) = vmem_call(
            solve_kernel,
            [jax.ShapeDtypeStruct((frames, rank), BF16)],
            [own_half, got_half, *cores],
            flops=5e9,
            where=where,
        )
        return [left, *rights]

    blocks = [0, *range(rows // 2, frames, rows), frames]
    sketch = run(
        functools.partial(first_kernel, blocks),
        1,
        [pl.BlockSpec(memory_space=pltpu.HBM)] * 3,
        sketch_specs,
        sketch_shapes,
        [pltpu.VMEM(x.shape, BF16) for x in (movie, vpt, fpt)] + sums + [pltpu.SemaphoreType.DMA((len(blocks) + 1,))],
        2,
        tuple(pltpu.with_memory_space_constraint(x, pltpu.HBM) for x in (movie, vpt, fpt)),
        limit=44 * 1024 * 1024,
    )
    sides = share_sketch(*sketch)
    for _ in range(1, ITERS):
        sketch = run(
            functools.partial(middle_kernel, n_row, chunk),
            frames // mid_rows,
            [resident, resident, block_cols(rank, mid_rows)] + side_specs,
            sketch_specs,
            sketch_shapes,
            [right, pltpu.VMEM((mid_rows, voxels), BF16)] + sums,
            3,
            (movie, vpt, fpt, *sides),
        )
        sides = share_sketch(*sketch)
    out = jax.ShapeDtypeStruct((frames, voxels), BF16)
    starts = [*range(0, frames, rows // 2), frames]
    return tuple(
        run(
            functools.partial(last_kernel, n_row, chunk, starts),
            1,
            [resident] + side_specs,
            [pl.BlockSpec(memory_space=pltpu.HBM)] * 2,
            [out, out],
            [right, pltpu.VMEM(out.shape, BF16), pltpu.VMEM(out.shape, BF16)]
            + [pltpu.SemaphoreType.DMA((len(starts) - 1, 2))],
            1,
            (movie, *sides),
            limit=32 * 1024 * 1024,
        )
    )


def solution(mesh):
    return jax.shard_map(
        on_device,
        mesh=mesh,
        in_specs=(P("frm", "vox"), P("vox", None), P("frm", None)),
        out_specs=(P("frm", "vox"), P("frm", "vox")),
        check_vma=False,
    )
```

```python
import functools

import jax
import jax.numpy as jnp
from jax import lax
from jax.experimental import pallas as pl
from jax.experimental.pallas import tpu as pltpu
from jax.sharding import PartitionSpec as P

ITERS = 2
cutoff = 1.0
ridge_scale = 0.1


F32 = jnp.float32
BF16 = jnp.bfloat16
LANES = 128


def dot(a, b, contract=((1,), (0,))):
    return lax.dot_general(a, b, (contract, ((), ())), preferred_element_type=F32)


def split2(x):
    high = x.astype(BF16)
    return high, (x - high.astype(F32)).astype(BF16)


def pack_core(core):
    high, low = split2(core)
    return jnp.concatenate([high, low], axis=1)


def unpack_core(packed):
    rank = packed.shape[0]
    wide = packed.astype(F32)
    return wide[:, :rank] + wide[:, rank:]


def finish_sketch(where_ref, y1_scr, y2_scr, vpt_ref, own_ref, send_ref, y2_refs):
    rank, frames = y1_scr.shape
    half = frames // 2
    peers = len(y2_refs)
    share = y2_scr.shape[1] // peers
    y2 = y2_scr[...]
    high, rest = split2(y2)
    low = (y2 - high.astype(F32) - rest.astype(F32)).astype(BF16)
    vp = vpt_ref[...]
    parts = dot(jnp.concatenate([high, rest, low], axis=0), vp, ((1,), (1,)))
    core = parts[:rank] + parts[rank : 2 * rank] + parts[2 * rank :]
    side = where_ref[0]
    row = where_ref[1]
    own_ref[:, :half] = y1_scr[:, pl.ds(pl.multiple_of(side * half, LANES), half)]
    own_ref[:, half : half + 2 * rank] = jnp.concatenate([core, jnp.zeros_like(core)], axis=1)
    other = y1_scr[:, pl.ds(pl.multiple_of((1 - side) * half, LANES), half)]
    send_ref[:, :half] = other.astype(BF16)
    send_ref[:, half : half + 2 * rank] = pack_core(core)
    for k in range(peers):
        slot = jnp.bitwise_xor(row, k)
        part = y2_scr[:, pl.ds(pl.multiple_of(slot * share, LANES), share)]
        y2_refs[k][...] = part.astype(y2_refs[k].dtype)


def first_kernel(blocks, where_ref, movie_ref, vpt_hbm, fpt_hbm, own_ref, send_ref, *rest):
    *y2_refs, held, vpt_ref, fpt_ref, y1_scr, y2_scr, sems = rest
    spans = [slice(start, stop) for start, stop in zip(blocks, blocks[1:])]
    copies = [
        pltpu.make_async_copy(movie_ref.at[span, :], held.at[span, :], sems.at[i]) for i, span in enumerate(spans)
    ]
    probes = [
        pltpu.make_async_copy(fpt_hbm, fpt_ref, sems.at[len(spans)]),
        pltpu.make_async_copy(vpt_hbm, vpt_ref, sems.at[len(spans) + 1]),
    ]
    for copy in [copies[0], *probes, *copies[1:]]:
        copy.start()
    for copy in probes:
        copy.wait()
    for i, span in enumerate(spans):
        copies[i].wait()
        cur = held[span, :]
        part = dot(fpt_ref[:, span], cur)
        y2_scr[...] = part if i == 0 else y2_scr[...] + part
        y1_scr[:, span] = dot(vpt_ref[...], cur, ((1,), (1,)))
    finish_sketch(where_ref, y1_scr, y2_scr, vpt_ref, own_ref, send_ref, y2_refs)


def pair_kernel(own_ref, got_ref, msg_ref):
    rank, width = own_ref.shape
    half = width - 2 * rank
    msg_ref[:, :half] = (own_ref[:, :half] + got_ref[:, :half].astype(F32)).astype(BF16)
    core = own_ref[:, half:][:, :rank] + unpack_core(got_ref[:, half:])
    msg_ref[:, half:] = pack_core(core)


def plane_kernel(*refs):
    *plane_refs, half_ref, core_ref = refs
    half = half_ref.shape[1]
    total = plane_refs[0][:, :half].astype(F32)
    core = unpack_core(plane_refs[0][:, half:])
    for ref in plane_refs[1:]:
        total += ref[:, :half].astype(F32)
        core += unpack_core(ref[:, half:])
    core_ref[...] = pack_core(core)
    half_ref[...] = total.astype(BF16)


def add_kernel(*refs):
    *parts, sum_ref = refs
    total = parts[0][...]
    for ref in parts[1:]:
        total += ref[...].astype(F32)
    sum_ref[...] = total.astype(BF16)


def solve_mixer(core):
    rank = core.shape[0]
    gram = lax.dot_general(
        core, core, (((0,), (0,)), ((), ())), precision=lax.Precision.HIGHEST, preferred_element_type=F32
    )
    r = lax.broadcasted_iota(jnp.int32, (rank, rank), 0)
    c = lax.broadcasted_iota(jnp.int32, (rank, rank), 1)
    eye = (r == c).astype(F32)
    scale = 1.0 / (jnp.sum(gram * eye) / rank + 1e-06)
    table = jnp.concatenate([gram * scale + ridge_scale * eye, core.T * scale], axis=1)
    width = table.shape[1]
    tall = 8
    tile = (tall, width)
    line = lax.broadcasted_iota(jnp.int32, tile, 0)
    tiles = [table[i : i + tall, :] for i in range(0, rank, tall)]
    for k in range(0, rank, 4):
        own, i = k // tall, k % tall
        cols = [[jnp.broadcast_to(t[:, k + j : k + j + 1], tile) for t in tiles] for j in range(4)]
        row = lambda t, j: jnp.broadcast_to(t[i + j : i + j + 1, :], tile)
        at = lambda m, j: row(cols[j][own], m)
        r0, r1, r2, r3 = [row(tiles[own], j) for j in range(4)]
        a, b, d = at(0, 0), at(1, 0), at(1, 1)
        e0, e1, f0, f1 = at(2, 0), at(2, 1), at(3, 0), at(3, 1)
        det = a * d - b * b
        w0, w1, z0, z1 = d * e0 - b * e1, a * e1 - b * e0, d * f0 - b * f1, a * f1 - b * f0
        p = at(2, 2) * det - (e0 * w0 + e1 * w1)
        q = at(3, 2) * det - (e0 * z0 + e1 * z1)
        t = at(3, 3) * det - (f0 * z0 + f1 * z1)
        inv, inv_late = 1.0 / det, det * (1.0 / (p * t - q * q))
        n0, n1 = (r0 * d - r1 * b) * inv, (r1 * a - r0 * b) * inv
        s2, s3 = r2 - (e0 * n0 + e1 * n1), r3 - (f0 * n0 + f1 * n1)
        n2, n3 = (s2 * t - s3 * q) * inv_late, (s3 * p - s2 * q) * inv_late
        n0 = n0 - (w0 * n2 + z0 * n3) * inv
        n1 = n1 - (w1 * n2 + z1 * n3) * inv
        for j in range(4):
            cols[j][own] = cols[j][own] - (line == i + j).astype(F32)
        tiles = [
            x - ((c0 * n0 + c1 * n1) + (c2 * n2 + c3 * n3)) for x, c0, c1, c2, c3 in zip(tiles, *cols)
        ]
    return jnp.concatenate(tiles, axis=0)[:, rank:]


def solve_kernel(where_ref, own_half_ref, got_half_ref, *rest):
    *core_refs, left_ref = rest
    half = own_half_ref.shape[1]
    core = unpack_core(core_refs[0][...])
    for ref in core_refs[1:]:
        core += unpack_core(ref[...])
    high, low = split2(solve_mixer(core))
    side = where_ref[0]
    for k, ref in enumerate((own_half_ref, got_half_ref)):
        y1 = ref[...]
        left = dot(y1, high, ((0,), (0,))) + dot(y1, low, ((0,), (0,)))
        slot = jnp.bitwise_xor(side, k)
        left_ref[pl.ds(pl.multiple_of(slot * half, half), half), :] = left.astype(BF16)


def join_right(where_ref, right_refs, right_scr):
    share = right_refs[0].shape[1]
    for k, ref in enumerate(right_refs):
        slot = jnp.bitwise_xor(where_ref[1], k)
        right_scr[:, pl.ds(pl.multiple_of(slot * share, LANES), share)] = ref[...]


def middle_kernel(n_row, chunk, where_ref, movie_ref, vpt_ref, fpt_ref, left_ref, *rest):
    right_refs = rest[:n_row]
    own_ref, send_ref = rest[n_row : 2 + n_row]
    *y2_refs, right_scr, cur_scr, y1_scr, y2_scr = rest[2 + n_row :]
    step = pl.program_id(0)
    rows, voxels = cur_scr.shape

    @pl.when(step == 0)
    def _():
        join_right(where_ref, right_refs, right_scr)
        y2_scr[...] = jnp.zeros_like(y2_scr)

    span = pl.ds(pl.multiple_of(step * rows, rows), rows)
    left = left_ref[span, :]
    fpt = fpt_ref[...]
    cols = [slice(j, j + chunk) for j in range(0, voxels, chunk)]
    bound = jnp.asarray(cutoff, BF16)

    def sketch(c, y1):
        cur = cur_scr[:, c]
        y2_scr[:, c] += dot(fpt, cur)
        part = dot(vpt_ref[:, c], cur, ((1,), (1,)))
        return part if y1 is None else y1 + part

    y1 = None
    ahead = dot(left, right_scr[:, cols[0]])
    for j, c in enumerate(cols):
        low = ahead.astype(BF16)
        if j + 1 < len(cols):
            ahead = dot(left, right_scr[:, cols[j + 1]])
        cur_scr[:, c] = low + jnp.clip(movie_ref[span, c] - low, -bound, bound)
        if j > 0:
            y1 = sketch(cols[j - 1], y1)
    y1_scr[:, span] = sketch(cols[-1], y1)

    @pl.when(step == pl.num_programs(0) - 1)
    def _():
        finish_sketch(where_ref, y1_scr, y2_scr, vpt_ref, own_ref, send_ref, y2_refs)


def last_kernel(n_row, chunk, blocks, where_ref, movie_ref, left_ref, *rest):
    right_refs = rest[:n_row]
    low_ref, sparse_ref, right_scr, low_scr, sparse_scr, sems = rest[n_row:]
    voxels = low_scr.shape[1]
    join_right(where_ref, right_refs, right_scr)
    cols = [slice(j, j + chunk) for j in range(0, voxels, chunk)]
    copies = []
    for i, span in enumerate(slice(start, stop) for start, stop in zip(blocks, blocks[1:])):
        left = left_ref[span, :]
        ahead = dot(left, right_scr[:, cols[0]])
        for j, c in enumerate(cols):
            low = ahead
            if j + 1 < len(cols):
                ahead = dot(left, right_scr[:, cols[j + 1]])
            low_scr[span, c] = low.astype(BF16)
            gap = movie_ref[span, c].astype(F32) - low
            sparse_scr[span, c] = (gap - jnp.clip(gap, -cutoff, cutoff)).astype(BF16)
        for k, (scr, ref) in enumerate(((low_scr, low_ref), (sparse_scr, sparse_ref))):
            copies.append(pltpu.make_async_copy(scr.at[span, :], ref.at[span, :], sems.at[i, k]))
            copies[-1].start()
    for copy in copies:
        copy.wait()


def block_cols(rank, rows):
    return pl.BlockSpec((rank, rows), lambda i, *_: (0, i))


def size_of(arrays):
    return sum(a.size * a.dtype.itemsize for a in arrays)


def vmem_call(kernel, outs, args, flops=1e6, where=None):
    resident = pl.BlockSpec(memory_space=pltpu.VMEM)
    return pl.pallas_call(
        kernel,
        out_shape=outs,
        in_specs=([] if where is None else [pl.BlockSpec(memory_space=pltpu.SMEM)]) + [resident] * len(args),
        out_specs=[resident] * len(outs),
        compiler_params=pltpu.CompilerParams(vmem_limit_bytes=8 * 1024 * 1024),
        cost_estimate=pl.CostEstimate(flops=int(flops), bytes_accessed=size_of([*args, *outs]), transcendentals=0),
    )(*([] if where is None else [where]), *args)


def exchange(x, axis, k):
    size = lax.axis_size(axis)
    return lax.ppermute(x, axis, [(i, i ^ k) for i in range(size)])


def on_device(movie, voxel_probe, frame_probe):
    frames, voxels = movie.shape
    rank = voxel_probe.shape[1]
    n_vox, n_row = lax.axis_size("vox"), lax.axis_size("frm")
    half, share = frames // 2, voxels // n_row
    width = half + 2 * rank
    rows = min(512, frames)
    mid_rows = frames
    chunk = min(256, voxels)
    where = jnp.stack([lax.axis_index("vox") % 2, lax.axis_index("frm")]).astype(jnp.int32)
    vpt, fpt = voxel_probe.T, frame_probe.T

    resident = pl.BlockSpec(memory_space=pltpu.VMEM)
    sketch_shapes = [
        jax.ShapeDtypeStruct((rank, width), F32),
        jax.ShapeDtypeStruct((rank, width), BF16),
        jax.ShapeDtypeStruct((rank, share), F32),
    ] + [jax.ShapeDtypeStruct((rank, share), BF16)] * (n_row - 1)
    sketch_specs = [resident] * len(sketch_shapes)
    sums = [pltpu.VMEM((rank, frames), F32), pltpu.VMEM((rank, voxels), F32)]
    right = pltpu.VMEM((rank, voxels), BF16)
    probe_specs = [resident, block_cols(rank, rows)]
    side_specs = [resident] * (1 + n_row)

    def run(kernel, steps, in_specs, out_specs, out_shape, scratch, passes, args, limit=20 * 1024 * 1024):
        return pl.pallas_call(
            kernel,
            grid_spec=pltpu.PrefetchScalarGridSpec(
                num_scalar_prefetch=1,
                grid=(steps,),
                in_specs=in_specs,
                out_specs=out_specs,
                scratch_shapes=scratch,
            ),
            out_shape=out_shape,
            compiler_params=pltpu.CompilerParams(
                dimension_semantics=("arbitrary",), vmem_limit_bytes=limit
            ),
            cost_estimate=pl.CostEstimate(
                flops=2 * passes * frames * voxels * rank, bytes_accessed=2 * frames * voxels, transcendentals=0
            ),
        )(where, *args)

    def share_sketch(own, send, *y2_parts):
        got = exchange(send, "vox", 1)
        (msg,) = vmem_call(pair_kernel, [jax.ShapeDtypeStruct((rank, width), BF16)], [own, got])
        plane = [msg] + [exchange(msg, "vox", 2 * k) for k in range(1, n_vox // 2)]
        parts = [y2_parts[0]] + [exchange(y2_parts[k], "frm", k) for k in range(1, n_row)]
        own_half, core = vmem_call(
            plane_kernel,
            [jax.ShapeDtypeStruct((rank, half), BF16), jax.ShapeDtypeStruct((rank, 2 * rank), BF16)],
            plane,
        )
        cores = [core] + [exchange(core, "frm", k) for k in range(1, n_row)]
        got_half = exchange(own_half, "vox", 1)
        (mine,) = vmem_call(add_kernel, [jax.ShapeDtypeStruct((rank, share), BF16)], parts)
        rights = [mine] + [exchange(mine, "frm", k) for k in range(1, n_row)]
        (left,) = vmem_call(
            solve_kernel,
            [jax.ShapeDtypeStruct((frames, rank), BF16)],
            [own_half, got_half, *cores],
            flops=5e9,
            where=where,
        )
        return [left, *rights]

    blocks = [0, *range(rows // 2, frames, rows), frames]
    sketch = run(
        functools.partial(first_kernel, blocks),
        1,
        [pl.BlockSpec(memory_space=pltpu.HBM)] * 3,
        sketch_specs,
        sketch_shapes,
        [pltpu.VMEM(x.shape, BF16) for x in (movie, vpt, fpt)] + sums + [pltpu.SemaphoreType.DMA((len(blocks) + 1,))],
        2,
        tuple(pltpu.with_memory_space_constraint(x, pltpu.HBM) for x in (movie, vpt, fpt)),
        limit=44 * 1024 * 1024,
    )
    sides = share_sketch(*sketch)
    for _ in range(1, ITERS):
        sketch = run(
            functools.partial(middle_kernel, n_row, chunk),
            frames // mid_rows,
            [resident, resident, block_cols(rank, mid_rows)] + side_specs,
            sketch_specs,
            sketch_shapes,
            [right, pltpu.VMEM((mid_rows, voxels), BF16)] + sums,
            3,
            (movie, vpt, fpt, *sides),
        )
        sides = share_sketch(*sketch)
    out = jax.ShapeDtypeStruct((frames, voxels), BF16)
    starts = [*range(0, frames, rows // 2), frames]
    return tuple(
        run(
            functools.partial(last_kernel, n_row, chunk, starts),
            1,
            [resident] + side_specs,
            [pl.BlockSpec(memory_space=pltpu.HBM)] * 2,
            [out, out],
            [right, pltpu.VMEM(out.shape, BF16), pltpu.VMEM(out.shape, BF16)]
            + [pltpu.SemaphoreType.DMA((len(starts) - 1, 2))],
            1,
            (movie, *sides),
            limit=32 * 1024 * 1024,
        )
    )


def solution(mesh):
    return jax.shard_map(
        on_device,
        mesh=mesh,
        in_specs=(P("frm", "vox"), P("vox", None), P("frm", None)),
        out_specs=(P("frm", "vox"), P("frm", "vox")),
        check_vma=False,
    )
```
